1024 devices in a mesh: dp: 4 (over y), expert: 32 (over x, z_hi, core), tensor: 8 (over z_lo).
Axes of the slice: x: 4, y: 4, z: 32 (z_hi: 4, z_lo: 8; z = z_hi * 8 + z_lo), core: 2. Of those that a mesh axis runs over, the one named last changes fastest.
Arguments:
- hidden: bfloat16 [16384, 2048], P(('dp', 'expert')), may hold values from -6 to 6
- out_grad: bfloat16 [16384, 7168], P(('dp', 'expert'), 'tensor'), may hold values from -6 to 6
- w_down: bfloat16 [32, 2048, 7168], P('expert', None, 'tensor'), may hold values from -0.125 to 0.125
- routes: int32 [16384, 1], P(('dp', 'expert')), may hold values from 0 to 31; in each aligned block of 128 rows (0 to 127, 128 to 255, ...) at most 8 rows name the same one
- placement: int32 [32], replicated, may hold values from 0 to 31, as said below
Outputs:
- output: bfloat16 [16384, 7168], P(('dp', 'expert'), 'tensor')
- d_hidden: bfloat16 [16384, 2048], P(('dp', 'expert'), 'tensor')
- d_weight: bfloat16 [32, 2048, 7168], P('expert', 'dp', 'tensor')
The draws below stay inside these ranges and needn't reach their ends.
Inputs may be any that keep to these rules, and one draw needn't show every extreme that they name: `routes`: among the 128 tokens of one index pair of dp and expert, no expert is named more than 8 times, a bound that some block reaches. `placement`: each expert is held at exactly one index.
All inputs are finite; a program needn't handle non-finite values.
Results may differ from the reference program's by a relative error of at most 0.009.
Values may be sent and summed in bfloat16 or wider, within the bound.
A program may use at most 32 MiB of HBM per device.

```python
import math
import jax
import jax.numpy as jnp
import numpy as np
from jax import lax

D = 7168
FF = 2048
TOK_DEV = 128
EXPERTS = 32
CAP = 8
TOKENS = 16384
N_DP = 4
N_EXPERT = 32


def draw_placement(key, part):
    return jax.random.permutation(jax.random.fold_in(key, 7919), EXPERTS).astype(jnp.int32)


def block_scale(stream_key, dims, cuts, smallest, high):
    loudness, own = 1.0, jax.random.fold_in(stream_key, 6)
    for axis_at, parts in cuts:
        heights = jnp.exp(jax.random.uniform(jax.random.fold_in(own, axis_at), (parts,), jnp.float32, smallest / len(cuts), high / len(cuts)))
        loudness = loudness * jnp.repeat(heights, dims[axis_at] // parts).reshape([-1 if axis == axis_at else 1 for axis in range(len(dims))])
    return loudness


def assign_block(rng, own, number, rows, amount, top, most, lean):
    ranking = jax.random.permutation(rng, amount)
    heavy_load, ordinary = load_shares(amount, rows * top, most, lean, True), load_shares(amount, rows * top, most, lean, False)
    places = jnp.arange(amount)

    def named(lengths, turn):
        used = int((lengths > 0).sum())
        fixed = max(1, used // 4)
        moved = fixed + (places - fixed + turn * (used - fixed)) % max(1, amount - fixed)
        return jnp.zeros((amount,), jnp.int32).at[ranking[jnp.where(places < fixed, places, moved)]].set(jnp.asarray(lengths, jnp.int32))

    lengths = jnp.where(number % 4 == 0, named(heavy_load, number // 4), named(ordinary, number - number // 4 - 1))
    mixed = jax.random.permutation(jax.random.fold_in(own, 3), amount)
    giver, taker = mixed[0:amount // 2 * 2:2], mixed[1:amount // 2 * 2:2]
    margin = jnp.minimum(lengths[giver] - 1, most - lengths[taker]) // 2
    margin = jnp.where((giver == ranking[0]) | (taker == ranking[0]) | (lengths[taker] == 0), 0, jnp.maximum(margin, 0))
    moved = jax.random.randint(jax.random.fold_in(own, 4), (amount // 2,), 0, 1 << 20) % (margin + 1)
    lengths = lengths.at[giver].add(-moved).at[taker].add(moved)
    labels = jnp.searchsorted(jnp.cumsum(lengths), jnp.arange(rows * top), side="right").astype(jnp.int32)
    listing = labels.reshape(top, rows).T
    listing = listing[jax.random.permutation(jax.random.fold_in(own, 1), rows)]
    turn = jax.random.randint(jax.random.fold_in(own, 2), (rows, 1), 0, top)
    return jnp.take_along_axis(listing, (jnp.arange(top)[None, :] + turn) % top, axis=1)


def load_shares(number_of, total, most, lean, full):
    loads = [(1 << 20) // math.isqrt(rank ** lean) + 1 for rank in range(1, number_of + 1)]
    largest = most if full else min(most, max(-(-total // number_of), total * loads[0] // sum(loads)))
    least = 1 if total - largest >= number_of - 1 else 0
    given, rest = [largest] + [least] * (number_of - 1), total - largest - least * (number_of - 1)
    while rest > 0:
        free = [i for i in range(1, number_of) if given[i] < largest] or [i for i in range(1, number_of) if given[i] < most]
        whole, left = sum([loads[i] for i in free]), rest
        for i in free:
            extra = min(most - given[i], max(1, left * loads[i] // whole), rest)
            given[i] = given[i] + extra
            rest = rest - extra
    return np.array(given)


def centred(stream_key, extent, width, most, split=(), kind=jnp.bfloat16):
    entries = jax.random.normal(stream_key, extent, jnp.float32) * width
    if len(split) > 0:
        entries = block_scale(stream_key, extent, split, -0.22, 0.18) * entries
    return jnp.clip(entries, min=-most, max=most).astype(kind)


def setup_inputs(seed: int = 0) -> dict:
    seeds = jax.random.split(jax.random.key(seed), 6)
    hidden = centred(seeds[0], (TOKENS, FF), 1.0, 6.0, ((0, 128),))
    out_grad = centred(seeds[1], (TOKENS, D), 1.0, 6.0, ((0, 128), (1, 8)))
    w_down = centred(seeds[2], (EXPERTS, FF, D), FF ** -0.5, 0.125, ((0, 32), (2, 8)))
    routes_keys = jax.random.split(jax.random.fold_in(seeds[3], 1), TOKENS // TOK_DEV)
    routes_turns = jax.random.permutation(jax.random.fold_in(seeds[3], 3), TOKENS // TOK_DEV)
    routes = jax.vmap(lambda own, number: assign_block(jax.random.fold_in(seeds[3], 2), own, number, TOK_DEV, EXPERTS, 1, CAP, 2))(routes_keys, routes_turns).reshape((TOKENS, 1))
    placement = draw_placement(jax.random.fold_in(seeds[5], 71), 0)
    return dict(hidden=hidden, out_grad=out_grad, w_down=w_down, routes=routes, placement=placement)


def reference(hidden, out_grad, w_down, routes, placement):
    per = TOKENS // N_DP
    limit = N_EXPERT * CAP
    slot = jnp.take(placement, routes[:, 0]).astype(jnp.int32)
    slot_groups = slot.reshape(N_DP, per)
    hidden_pad = jnp.concatenate([hidden.reshape(N_DP, per, FF), jnp.zeros((N_DP, 1, FF), hidden.dtype)], axis=1)
    grad_pad = jnp.concatenate([out_grad.reshape(N_DP, per, D), jnp.zeros((N_DP, 1, D), out_grad.dtype)], axis=1)

    def expert(s):
        weight = w_down[s]
        total = jnp.zeros((FF, D), jnp.float32)
        outs, grads, places = [], [], []
        for group in range(N_DP):
            index = jnp.nonzero(slot_groups[group] == s, size=limit, fill_value=per)[0].astype(jnp.int32)
            rows_h = hidden_pad[group][index]
            rows_g = grad_pad[group][index]
            outs.append(jnp.dot(rows_h, weight, preferred_element_type=jnp.float32).astype(jnp.bfloat16))
            grads.append(jnp.dot(rows_g, weight.T, preferred_element_type=jnp.float32).astype(jnp.bfloat16))
            part = jnp.dot(rows_h.T, rows_g, preferred_element_type=jnp.float32).astype(jnp.bfloat16)
            total = total + part.astype(jnp.float32)
            places.append(jnp.where(index == per, TOKENS, index + group * per).astype(jnp.int32))
        return jnp.stack(outs), jnp.stack(grads), jnp.stack(places), total.astype(jnp.bfloat16)

    outs, grads, places, d_weight = lax.map(expert, jnp.arange(N_EXPERT, dtype=jnp.int32))
    flat = places.reshape(-1)
    output = jnp.zeros((TOKENS, D), jnp.bfloat16).at[flat].set(outs.reshape(-1, D), mode="drop")
    d_hidden = jnp.zeros((TOKENS, FF), jnp.bfloat16).at[flat].set(grads.reshape(-1, FF), mode="drop")
    return output, d_hidden, d_weight
```

```python
import jax
import jax.numpy as jnp
from jax import lax
from jax.sharding import PartitionSpec as P


def shards(hidden, out_grad, w_down, routes, placement):
    experts = lax.axis_size("expert")
    parts = lax.axis_size("tensor")
    tok = hidden.shape[0]
    width = hidden.shape[1]
    part = width // parts
    cols = out_grad.shape[1]
    cap = 2 * tok // experts
    slots = experts * cap
    chosen = routes == jnp.arange(placement.shape[0], dtype=jnp.int32)[None, :]
    target = jnp.sum(jnp.where(chosen, placement[None, :], 0), axis=1)
    landing = target[:, None] == jnp.arange(experts, dtype=jnp.int32)[None, :]
    counted = jnp.cumsum(landing.astype(jnp.int32), axis=0) - 1
    within = jnp.sum(jnp.where(landing, counted, 0), axis=1)
    position = target * cap + within
    picker = (jnp.arange(slots, dtype=jnp.int32)[:, None] == position[None, :]).astype(jnp.bfloat16)
    mine = lax.dynamic_slice_in_dim(hidden, lax.axis_index("tensor") * part, part, axis=1)
    rows = jnp.concatenate([out_grad, mine], axis=1)
    send = jnp.dot(picker, rows, preferred_element_type=jnp.float32).astype(jnp.bfloat16)
    recv = lax.all_to_all(
        send.reshape(experts, cap, -1), "expert", split_axis=0, concat_axis=0, tiled=True
    ).reshape(slots, -1)
    slot_grad = recv[:, :cols]
    pieces = lax.all_gather(recv[:, cols:], "tensor", axis=0, tiled=False)
    slot_hidden = pieces.transpose(1, 0, 2).reshape(slots, width)
    weight = w_down[0]
    partial_value = lax.dot_general(
        slot_grad, weight, (((1,), (1,)), ((), ())), preferred_element_type=jnp.float32
    ).astype(jnp.bfloat16)
    hidden_grad = lax.psum_scatter(partial_value, "tensor", scatter_dimension=1, tiled=True)
    out_rows = jnp.dot(slot_hidden, weight, preferred_element_type=jnp.float32).astype(jnp.bfloat16)
    back = lax.all_to_all(
        jnp.concatenate([out_rows, hidden_grad], axis=1).reshape(experts, cap, -1),
        "expert",
        split_axis=0,
        concat_axis=0,
        tiled=True,
    ).reshape(slots, -1)
    final = jnp.einsum("rt,rd->td", picker, back, preferred_element_type=jnp.float32).astype(jnp.bfloat16)
    output = final[:, :cols]
    d_hidden = final[:, cols:]
    summed = lax.psum_scatter(
        lax.dot_general(
            slot_hidden, slot_grad, (((0,), (0,)), ((), ())), preferred_element_type=jnp.float32
        ).astype(jnp.bfloat16),
        "dp",
        scatter_dimension=0,
        tiled=True,
    )
    d_weight = summed[None]
    return (output, d_hidden, d_weight)


def solution(mesh):
    in_specs = (
        P(("dp", "expert"), None),
        P(("dp", "expert"), "tensor"),
        P("expert", None, "tensor"),
        P(("dp", "expert"), None),
        P(),
    )
    out_specs = (
        P(("dp", "expert"), "tensor"),
        P(("dp", "expert"), "tensor"),
        P("expert", "dp", "tensor"),
    )
    return jax.shard_map(shards, mesh=mesh, in_specs=in_specs, out_specs=out_specs, check_vma=False)
```

```python
import jax
import jax.numpy as jnp
from jax import lax
from jax.experimental import pallas as pl
from jax.experimental.pallas import tpu as pltpu
from jax.sharding import PartitionSpec as P

MESH = pl.DeviceIdType.MESH
F32 = jnp.float32
BF16 = jnp.bfloat16
NE = 32
CAP = 8
LINE = 8
UNITS = 24
SKEW = 3
SPLIT = 2
SKEW2 = 2


def exchange(
    send_h, send_g, w, out_recv, dh_recv, g_all, h_all,
    recv_h, recv_g, out_send, dh_send, partial, acc, plus_in, minus_in, plus_out, minus_out,
    g_ss, g_rs, o_ss, o_rs, d_ss, d_rs, h_ss, h_rs, x_ss, p_ss, p_rs, m_ss, m_rs,
    rp_ss, rp_rs, rm_ss, rm_rs, y_ss, y_rs, loc,
):
    e = lax.axis_index("expert")
    j = lax.axis_index("tensor")
    y = lax.axis_index("dp")
    width = send_h.shape[2]
    half = width // 2
    cols = send_g.shape[2]
    part = width // LINE
    quarter = width // 4
    x, h, c = e // 8, (e // 2) % 4, e % 2
    first, last = j == 0, j == LINE - 1

    def at(dx, dh, dc):
        return ((x + dx) % 4) * 8 + ((h + dh) % 4) * 2 + (c + dc) % 2

    def peer(k):
        q = k // 8
        dh = jnp.where(q == 0, 2, jnp.where(q == 1, 1, jnp.where(q == 2, 3, 0)))
        return at((k % 8) // 2, dh, k % 2)

    SELF = 24

    def others(fn):
        def step(k, carry):
            fn(k + (k >= SELF).astype(jnp.int32))
            return carry

        lax.fori_loop(0, NE - 1, step, 0)

    sign = jnp.where(last, 1, -1)
    far_end = jnp.where(last, 0, LINE - 1)
    at_end = jnp.logical_or(first, last)

    barrier = pltpu.get_barrier_semaphore()
    others(lambda k: pl.semaphore_signal(barrier, inc=1, device_id={"expert": peer(k)}, device_id_type=MESH))
    for d in (1, 2, 3):
        pl.semaphore_signal(barrier, inc=1, device_id={"dp": (y + d) % 4}, device_id_type=MESH)

    @pl.when(j > 0)
    def _():
        pl.semaphore_signal(barrier, inc=1, device_id={"tensor": j - 1}, device_id_type=MESH)

    @pl.when(j < LINE - 1)
    def _():
        pl.semaphore_signal(barrier, inc=1, device_id={"tensor": j + 1}, device_id_type=MESH)

    def partner(k):
        g = 1 + k // 8
        return ((k % 8) // 2) * 8 + ((h + sign * g + 8) % 4) * 2 + k % 2

    @pl.when(at_end)
    def _():
        def step(k, carry):
            pl.semaphore_signal(
                barrier, inc=1, device_id={"expert": partner(k), "tensor": far_end}, device_id_type=MESH
            )
            return carry

        lax.fori_loop(0, 16, step, 0)

    pl.semaphore_wait(barrier, 34 + (j > 0) + (j < LINE - 1) + jnp.where(at_end, 16, 0))

    def local(k, src, dst):
        return pltpu.make_async_copy(src, dst, loc.at[k])

    local(0, send_h.at[e], recv_h.at[e]).start()
    local(1, send_g.at[e], recv_g.at[e]).start()

    side = jnp.where(last, 0, 1)

    def export(k, recv):
        r, piece = k % 8, k // 8
        t = ((r // 2) * 8) + ((h + sign * jnp.where(piece == 0, 2, 1) + 8) % 4) * 2 + r % 2
        col = jnp.where(piece == 0, side, piece - 1)
        mine = x * 2 + c
        unit = jnp.where(piece == 0, 16 + mine, mine * 2 + piece - 1)
        span = pl.ds(pl.multiple_of(col * half, half), half)
        return pltpu.make_async_remote_copy(
            src_ref=send_h.at[t, :, span],
            dst_ref=recv_h.at[e, :, span],
            send_sem=x_ss.at[k],
            recv_sem=recv.at[unit],
            device_id={"expert": t, "tensor": far_end},
            device_id_type=MESH,
        )

    def run(count, fn):
        def step(k, carry):
            fn(k)
            return carry

        lax.fori_loop(0, count, step, 0)

    @pl.when(last)
    def _():
        run(UNITS, lambda k: export(k, p_rs).start())

    @pl.when(first)
    def _():
        run(UNITS, lambda k: export(k, m_rs).start())

    def near(k):
        t = at(k // 2, 0, k % 2)
        return pltpu.make_async_remote_copy(
            src_ref=send_h.at[t],
            dst_ref=recv_h.at[e],
            send_sem=h_ss.at[k],
            recv_sem=h_rs.at[x * 2 + c],
            device_id={"expert": t},
            device_id_type=MESH,
        )

    run(7, lambda k: near(k + 1).start())

    def spread(src, dst, ss, rs):
        def copy(k):
            t = peer(k)
            return pltpu.make_async_remote_copy(
                src_ref=src.at[t],
                dst_ref=dst.at[e],
                send_sem=ss.at[k],
                recv_sem=rs.at[e],
                device_id={"expert": t},
                device_id_type=MESH,
            )

        return copy

    def arrivals(dst, rs):
        def copy(k):
            t = peer(k)
            pltpu.make_async_copy(dst.at[t], dst.at[t], rs.at[t]).wait()

        return copy

    grads = spread(send_g, recv_g, g_ss, g_rs)
    others(lambda k: grads(k).start())

    def relay(u, up):
        ss, rs = (p_ss, p_rs) if up else (m_ss, m_rs)
        wide = u < 16
        idx = jnp.where(wide, u // 2, u - 16)
        col = jnp.where(wide, u % 2, 0 if up else 1)
        hop = jnp.where(wide, 1, 2)
        g = (h - hop + 4) % 4 if up else (h + hop) % 4
        s = (idx // 2) * 8 + g * 2 + idx % 2
        ref = recv_h.at[s, :, pl.ds(pl.multiple_of(col * half, half), half)]
        return pltpu.make_async_remote_copy(
            src_ref=ref,
            dst_ref=ref,
            send_sem=ss.at[u],
            recv_sem=rs.at[u],
            device_id={"tensor": (j + 1) % LINE if up else (j + LINE - 1) % LINE},
            device_id_type=MESH,
        )

    def relay_step(tau):
        for up in (True, False):
            u = tau - SKEW * (j if up else LINE - 1 - j)

            @pl.when(jnp.logical_and(u >= 0, u < UNITS))
            def _(u=u, up=up):
                copy = relay(u, up)
                copy.wait_recv()

                @pl.when(j < LINE - 1 if up else j > 0)
                def _():
                    copy.start()

    run(UNITS + SKEW * (LINE - 1), relay_step)

    local(0, send_h.at[e], recv_h.at[e]).wait()

    def near_in(k):
        t = at((k + 1) // 2, 0, (k + 1) % 2)
        ref = recv_h.at[t]
        pltpu.make_async_copy(ref, ref, h_rs.at[(t // 8) * 2 + t % 2]).wait()

    run(7, near_in)

    def hid_y(d):
        t = (y + d) % 4
        return pltpu.make_async_remote_copy(
            src_ref=recv_h.at[:, :, pl.ds(pl.multiple_of(t * quarter, quarter), quarter)],
            dst_ref=h_all.at[y],
            send_sem=y_ss.at[d],
            recv_sem=y_rs.at[y],
            device_id={"dp": t},
            device_id_type=MESH,
        )

    def grad_y(d):
        return pltpu.make_async_remote_copy(
            src_ref=recv_g,
            dst_ref=g_all.at[y],
            send_sem=y_ss.at[4 + d],
            recv_sem=y_rs.at[4 + y],
            device_id={"dp": (y + d) % 4},
            device_id_type=MESH,
        )

    own_h = recv_h.at[:, :, pl.ds(pl.multiple_of(y * quarter, quarter), quarter)]
    for d in (2, 1, 3):
        hid_y(d).start()
    local(2, own_h, h_all.at[y]).start()

    rows = NE * CAP

    def project(start, size):
        span = pl.ds(start, size)
        value = jnp.dot(recv_h[...].reshape(rows, width), w[:, span], preferred_element_type=F32)
        out_send[:, :, span] = value.astype(BF16).reshape(NE, CAP, size)

    run(cols // 256, lambda k: project(pl.multiple_of(k * 256, 256), 256))
    if cols % 256:
        project(cols - cols % 256, cols % 256)
    outs = spread(out_send, out_recv, o_ss, o_rs)
    others(lambda k: outs(k).start())
    local(3, out_send.at[e], out_recv.at[e]).start()

    local(1, send_g.at[e], recv_g.at[e]).wait()
    others(arrivals(recv_g, g_rs))
    for d in (2, 1, 3):
        grad_y(d).start()
    local(4, recv_g, g_all.at[y]).start()

    def chunk(d):
        value = lax.dot_general(
            recv_g[...].reshape(rows, cols),
            w[pl.ds(pl.multiple_of(d * part, part), part), :],
            (((1,), (1,)), ((), ())),
            preferred_element_type=F32,
        )
        partial[d] = value

    run(LINE, chunk)
    acc[...] = partial[j]
    piece = rows // SPLIT

    def passing(m, up):
        inn, out, ss, rs = (plus_in, plus_out, rp_ss, rp_rs) if up else (minus_in, minus_out, rm_ss, rm_rs)
        return pltpu.make_async_remote_copy(
            src_ref=out.at[m],
            dst_ref=inn.at[m],
            send_sem=ss.at[m],
            recv_sem=rs.at[m],
            device_id={"tensor": (j + 1) % LINE if up else (j + LINE - 1) % LINE},
            device_id_type=MESH,
        )

    def reduce_step(tau):
        for up in (True, False):
            lag = j if up else LINE - 1 - j
            inn, out = (plus_in, plus_out) if up else (minus_in, minus_out)
            m = tau - SKEW2 * lag
            count = SPLIT * (LINE - lag)

            @pl.when(jnp.logical_and(m >= 0, m < count))
            def _(m=m, up=up, lag=lag, inn=inn, out=out, count=count):
                copy = passing(m, up)
                d = LINE - 1 - m // SPLIT if up else m // SPLIT
                span = pl.ds(pl.multiple_of((m % SPLIT) * piece, piece), piece)
                final = m >= count - SPLIT

                @pl.when(lag > 0)
                def _():
                    copy.wait_recv()

                    @pl.when(final)
                    def _():
                        acc[span, :] += inn[m].astype(F32)

                    @pl.when(jnp.logical_not(final))
                    def _():
                        out[m] = (partial[d, span, :] + inn[m].astype(F32)).astype(BF16)

                @pl.when(lag == 0)
                def _():
                    out[m] = partial[d, span, :].astype(BF16)

                @pl.when(jnp.logical_not(final))
                def _():
                    copy.start()

    run(max(SPLIT * (LINE - k) + SKEW2 * k for k in range(LINE)), reduce_step)
    dh_send[...] = acc[...].astype(BF16).reshape(NE, CAP, part)
    backs = spread(dh_send, dh_recv, d_ss, d_rs)
    others(lambda k: backs(k).start())
    local(5, dh_send.at[e], dh_recv.at[e]).start()

    local(2, own_h, h_all.at[y]).wait()
    local(3, out_send.at[e], out_recv.at[e]).wait()
    local(4, recv_g, g_all.at[y]).wait()
    local(5, dh_send.at[e], dh_recv.at[e]).wait()
    others(lambda k: grads(k).wait_send())
    others(lambda k: outs(k).wait_send())
    run(7, lambda k: near(k + 1).wait_send())

    @pl.when(last)
    def _():
        run(UNITS, lambda k: export(k, p_rs).wait_send())

    @pl.when(first)
    def _():
        run(UNITS, lambda k: export(k, m_rs).wait_send())

    @pl.when(j < LINE - 1)
    def _():
        run(UNITS, lambda u: relay(u, True).wait_send())
        run(SPLIT * (LINE - 1 - j), lambda m: passing(m, True).wait_send())

    @pl.when(j > 0)
    def _():
        run(UNITS, lambda u: relay(u, False).wait_send())
        run(SPLIT * j, lambda m: passing(m, False).wait_send())

    for d in (1, 2, 3):
        hid_y(d).wait_send()
        grad_y(d).wait_send()
        t = (y + d) % 4
        pltpu.make_async_copy(h_all.at[t], h_all.at[t], y_rs.at[t]).wait()
        pltpu.make_async_copy(g_all.at[t], g_all.at[t], y_rs.at[4 + t]).wait()
    others(arrivals(out_recv, o_rs))
    others(lambda k: backs(k).wait_send())
    others(arrivals(dh_recv, d_rs))


def shards(hidden, out_grad, w_down, routes, placement):
    experts = lax.axis_size("expert")
    replicas = lax.axis_size("dp")
    tok, width = hidden.shape
    cols = out_grad.shape[1]
    slots = experts * CAP
    part = width // LINE
    chosen = routes == jnp.arange(placement.shape[0], dtype=jnp.int32)[None, :]
    target = jnp.sum(jnp.where(chosen, placement[None, :], 0), axis=1)
    landing = target[:, None] == jnp.arange(experts, dtype=jnp.int32)[None, :]
    counted = jnp.cumsum(landing.astype(jnp.int32), axis=0) - 1
    within = jnp.sum(jnp.where(landing, counted, 0), axis=1)
    position = target * CAP + within
    picker = (jnp.arange(slots, dtype=jnp.int32)[:, None] == position[None, :]).astype(BF16)
    send_hidden = jnp.dot(picker, hidden, preferred_element_type=F32).astype(BF16)
    send_grad = jnp.dot(picker, out_grad, preferred_element_type=F32).astype(BF16)
    vmem = pl.BlockSpec(memory_space=pltpu.VMEM)
    dma = pltpu.SemaphoreType.DMA
    piece = (SPLIT * LINE, slots // SPLIT, part)
    back_out, back_grad, g_all, h_all = pl.pallas_call(
        exchange,
        out_shape=(
            jax.ShapeDtypeStruct((experts, CAP, cols), BF16),
            jax.ShapeDtypeStruct((experts, CAP, part), BF16),
            jax.ShapeDtypeStruct((replicas, experts, CAP, cols), BF16),
            jax.ShapeDtypeStruct((replicas, experts, CAP, width // replicas), BF16),
        ),
        in_specs=[vmem] * 3,
        out_specs=(vmem,) * 4,
        scratch_shapes=[
            pltpu.VMEM((experts, CAP, width), BF16),
            pltpu.VMEM((experts, CAP, cols), BF16),
            pltpu.VMEM((experts, CAP, cols), BF16),
            pltpu.VMEM((experts, CAP, part), BF16),
            pltpu.VMEM((LINE, slots, part), F32),
            pltpu.VMEM((slots, part), F32),
            pltpu.VMEM(piece, BF16),
            pltpu.VMEM(piece, BF16),
            pltpu.VMEM(piece, BF16),
            pltpu.VMEM(piece, BF16),
            *[dma((NE,))] * 6,
            *[dma((8,))] * 2,
            *[dma((UNITS,))] * 5,
            *[dma((SPLIT * LINE,))] * 4,
            *[dma((8,))] * 2,
            dma((6,)),
        ],
        compiler_params=pltpu.CompilerParams(collective_id=0, has_side_effects=True, vmem_limit_bytes=40 * 2**20),
        name="exchange",
    )(send_hidden.reshape(experts, CAP, width), send_grad.reshape(experts, CAP, cols), w_down[0])
    output = jnp.einsum("rt,rd->td", picker, back_out.reshape(slots, cols), preferred_element_type=F32).astype(BF16)
    d_hidden = jnp.einsum("rt,rd->td", picker, back_grad.reshape(slots, part), preferred_element_type=F32).astype(BF16)
    d_weight = lax.dot_general(
        h_all.reshape(replicas * slots, -1),
        g_all.reshape(replicas * slots, cols),
        (((0,), (0,)), ((), ())),
        preferred_element_type=F32,
    ).astype(BF16)
    return (output, d_hidden, d_weight[None])


def solution(mesh):
    in_specs = (
        P(("dp", "expert"), None),
        P(("dp", "expert"), "tensor"),
        P("expert", None, "tensor"),
        P(("dp", "expert"), None),
        P(),
    )
    out_specs = (
        P(("dp", "expert"), "tensor"),
        P(("dp", "expert"), "tensor"),
        P("expert", "dp", "tensor"),
    )
    return jax.shard_map(shards, mesh=mesh, in_specs=in_specs, out_specs=out_specs, check_vma=False)
```

```python
import jax
import jax.numpy as jnp
from jax import lax
from jax.experimental import pallas as pl
from jax.experimental.pallas import tpu as pltpu
from jax.sharding import PartitionSpec as P

MESH = pl.DeviceIdType.MESH
F32 = jnp.float32
BF16 = jnp.bfloat16
NE = 32
CAP = 8
LINE = 8
UNITS = 24
SKEW = 5
SPLIT = 2
SKEW2 = 2
START = 30
EXPORT_FIRST = True


def exchange(
    hidden, out_grad, picker, w_any, out_recv, dh_recv, g_all, h_all,
    send_h, send_g, w, recv_h, recv_g, out_send, dh_send, partial, acc, plus_in, minus_in, plus_out, minus_out,
    g_ss, g_rs, o_ss, o_rs, d_ss, d_rs, h_ss, h_rs, x_ss, p_ss, p_rs, m_ss, m_rs,
    rp_ss, rp_rs, rm_ss, rm_rs, y_ss, y_rs, loc,
):
    e = lax.axis_index("expert")
    j = lax.axis_index("tensor")
    y = lax.axis_index("dp")
    local_w = pltpu.make_async_copy(w_any, w, loc.at[6])
    local_w.start()
    width = send_h.shape[2]
    half = width // 2
    cols = send_g.shape[2]
    part = width // LINE
    quarter = width // 4
    x, h, c = e // 8, (e // 2) % 4, e % 2
    first, last = j == 0, j == LINE - 1

    def at(dx, dh, dc):
        return ((x + dx) % 4) * 8 + ((h + dh) % 4) * 2 + (c + dc) % 2

    def peer(k):
        q = k // 8
        dh = jnp.where(q == 0, 2, jnp.where(q == 1, 1, jnp.where(q == 2, 3, 0)))
        return at((k % 8) // 2, dh, k % 2)

    SELF = 24

    def others(fn):
        def step(k, carry):
            fn(k + (k >= SELF).astype(jnp.int32))
            return carry

        lax.fori_loop(0, NE - 1, step, 0)

    sign = jnp.where(last, 1, -1)
    far_end = jnp.where(last, 0, LINE - 1)
    at_end = jnp.logical_or(first, last)

    barrier = pltpu.get_barrier_semaphore()
    others(lambda k: pl.semaphore_signal(barrier, inc=1, device_id={"expert": peer(k)}, device_id_type=MESH))
    for d in (1, 2, 3):
        pl.semaphore_signal(barrier, inc=1, device_id={"dp": (y + d) % 4}, device_id_type=MESH)

    @pl.when(j > 0)
    def _():
        pl.semaphore_signal(barrier, inc=1, device_id={"tensor": j - 1}, device_id_type=MESH)

    @pl.when(j < LINE - 1)
    def _():
        pl.semaphore_signal(barrier, inc=1, device_id={"tensor": j + 1}, device_id_type=MESH)

    def partner(k):
        g = 1 + k // 8
        return ((k % 8) // 2) * 8 + ((h + sign * g + 8) % 4) * 2 + k % 2

    @pl.when(at_end)
    def _():
        def step(k, carry):
            pl.semaphore_signal(
                barrier, inc=1, device_id={"expert": partner(k), "tensor": far_end}, device_id_type=MESH
            )
            return carry

        lax.fori_loop(0, 16, step, 0)

    def pick(src, dst, start, size):
        span = pl.ds(start, size)
        value = jnp.dot(picker[...], src[:, span], preferred_element_type=F32)
        dst[:, :, span] = value.astype(BF16).reshape(NE, CAP, size)

    def pick_all(src, dst, total):
        def step(k, carry):
            pick(src, dst, pl.multiple_of(k * 256, 256), 256)
            return carry

        lax.fori_loop(0, total // 256, step, 0)
        if total % 256:
            pick(src, dst, total - total % 256, total % 256)

    pick_all(hidden, send_h, width)
    pick_all(out_grad, send_g, cols)

    pl.semaphore_wait(barrier, 34 + (j > 0) + (j < LINE - 1) + jnp.where(at_end, 16, 0))

    def local(k, src, dst):
        return pltpu.make_async_copy(src, dst, loc.at[k])

    local(0, send_h.at[e], recv_h.at[e]).start()
    local(1, send_g.at[e], recv_g.at[e]).start()

    side = jnp.where(last, 0, 1)

    def export(k, recv):
        r, piece = k % 8, k // 8
        t = ((r // 2) * 8) + ((h + sign * jnp.where(piece == 0, 2, 1) + 8) % 4) * 2 + r % 2
        col = jnp.where(piece == 0, side, piece - 1)
        mine = x * 2 + c
        unit = jnp.where(piece == 0, 16 + mine, mine * 2 + piece - 1)
        span = pl.ds(pl.multiple_of(col * half, half), half)
        return pltpu.make_async_remote_copy(
            src_ref=send_h.at[t, :, span],
            dst_ref=recv_h.at[e, :, span],
            send_sem=x_ss.at[k],
            recv_sem=recv.at[unit],
            device_id={"expert": t, "tensor": far_end},
            device_id_type=MESH,
        )

    def run(count, fn):
        def step(k, carry):
            fn(k)
            return carry

        lax.fori_loop(0, count, step, 0)

    def near(k):
        t = at(k // 2, 0, k % 2)
        return pltpu.make_async_remote_copy(
            src_ref=send_h.at[t],
            dst_ref=recv_h.at[e],
            send_sem=h_ss.at[k],
            recv_sem=h_rs.at[x * 2 + c],
            device_id={"expert": t},
            device_id_type=MESH,
        )

    def exports():
        @pl.when(last)
        def _():
            run(UNITS, lambda k: export(k, p_rs).start())

        @pl.when(first)
        def _():
            run(UNITS, lambda k: export(k, m_rs).start())

    def spread(src, dst, ss, rs):
        def copy(k):
            t = peer(k)
            return pltpu.make_async_remote_copy(
                src_ref=src.at[t],
                dst_ref=dst.at[e],
                send_sem=ss.at[k],
                recv_sem=rs.at[e],
                device_id={"expert": t},
                device_id_type=MESH,
            )

        return copy

    def arrivals(dst, rs):
        def copy(k):
            t = peer(k)
            pltpu.make_async_copy(dst.at[t], dst.at[t], rs.at[t]).wait()

        return copy

    grads = spread(send_g, recv_g, g_ss, g_rs)
    if EXPORT_FIRST:
        exports()
    others(lambda k: grads(k).start())
    if not EXPORT_FIRST:
        exports()
    run(7, lambda k: near(k + 1).start())

    def relay(u, up):
        ss, rs = (p_ss, p_rs) if up else (m_ss, m_rs)
        wide = u < 16
        idx = jnp.where(wide, u // 2, u - 16)
        col = jnp.where(wide, u % 2, 0 if up else 1)
        hop = jnp.where(wide, 1, 2)
        g = (h - hop + 4) % 4 if up else (h + hop) % 4
        s = (idx // 2) * 8 + g * 2 + idx % 2
        ref = recv_h.at[s, :, pl.ds(pl.multiple_of(col * half, half), half)]
        return pltpu.make_async_remote_copy(
            src_ref=ref,
            dst_ref=ref,
            send_sem=ss.at[u],
            recv_sem=rs.at[u],
            device_id={"tensor": (j + 1) % LINE if up else (j + LINE - 1) % LINE},
            device_id_type=MESH,
        )

    def relay_step(tau):
        for up in (True, False):
            u = tau - SKEW * (j if up else LINE - 1 - j)

            @pl.when(jnp.logical_and(u >= 0, u < UNITS))
            def _(u=u, up=up):
                copy = relay(u, up)
                copy.wait_recv()

                @pl.when(j < LINE - 1 if up else j > 0)
                def _():
                    copy.start()

    def near_in(k):
        t = at((k + 1) // 2, 0, (k + 1) % 2)
        ref = recv_h.at[t]
        pltpu.make_async_copy(ref, ref, h_rs.at[(t // 8) * 2 + t % 2]).wait()

    def hid_y(d):
        t = (y + d) % 4
        return pltpu.make_async_remote_copy(
            src_ref=recv_h.at[:, :, pl.ds(pl.multiple_of(t * quarter, quarter), quarter)],
            dst_ref=h_all.at[y],
            send_sem=y_ss.at[d],
            recv_sem=y_rs.at[y],
            device_id={"dp": t},
            device_id_type=MESH,
        )

    def grad_y(d):
        return pltpu.make_async_remote_copy(
            src_ref=recv_g,
            dst_ref=g_all.at[y],
            send_sem=y_ss.at[4 + d],
            recv_sem=y_rs.at[4 + y],
            device_id={"dp": (y + d) % 4},
            device_id_type=MESH,
        )

    own_h = recv_h.at[:, :, pl.ds(pl.multiple_of(y * quarter, quarter), quarter)]
    rows = NE * CAP

    def project(start, size):
        span = pl.ds(start, size)
        value = jnp.dot(recv_h[...].reshape(rows, width), w[:, span], preferred_element_type=F32)
        out_send[:, :, span] = value.astype(BF16).reshape(NE, CAP, size)

    outs = spread(out_send, out_recv, o_ss, o_rs)

    def forward():
        local(0, send_h.at[e], recv_h.at[e]).wait()
        run(7, near_in)
        run(cols // 256, lambda k: project(pl.multiple_of(k * 256, 256), 256))
        if cols % 256:
            project(cols - cols % 256, cols % 256)
        others(lambda k: outs(k).start())
        local(3, out_send.at[e], out_recv.at[e]).start()
        for d in (2, 1, 3):
            hid_y(d).start()
        local(2, own_h, h_all.at[y]).start()

    def chunk(d):
        value = lax.dot_general(
            recv_g[...].reshape(rows, cols),
            w[pl.ds(pl.multiple_of(d * part, part), part), :],
            (((1,), (1,)), ((), ())),
            preferred_element_type=F32,
        )
        partial[d] = value

    def backward():
        local(1, send_g.at[e], recv_g.at[e]).wait()
        others(arrivals(recv_g, g_rs))
        run(LINE, chunk)
        acc[...] = partial[j]
        for d in (2, 1, 3):
            grad_y(d).start()
        local(4, recv_g, g_all.at[y]).start()

    piece = rows // SPLIT

    def passing(m, up):
        inn, out, ss, rs = (plus_in, plus_out, rp_ss, rp_rs) if up else (minus_in, minus_out, rm_ss, rm_rs)
        return pltpu.make_async_remote_copy(
            src_ref=out.at[m],
            dst_ref=inn.at[m],
            send_sem=ss.at[m],
            recv_sem=rs.at[m],
            device_id={"tensor": (j + 1) % LINE if up else (j + LINE - 1) % LINE},
            device_id_type=MESH,
        )

    def reduce_step(tau):
        for up in (True, False):
            lag = j if up else LINE - 1 - j
            inn, out = (plus_in, plus_out) if up else (minus_in, minus_out)
            m = tau - SKEW2 * lag
            count = SPLIT * (LINE - lag)

            @pl.when(jnp.logical_and(m >= 0, m < count))
            def _(m=m, up=up, lag=lag, inn=inn, out=out, count=count):
                copy = passing(m, up)
                d = LINE - 1 - m // SPLIT if up else m // SPLIT
                span = pl.ds(pl.multiple_of((m % SPLIT) * piece, piece), piece)
                final = m >= count - SPLIT

                @pl.when(lag > 0)
                def _():
                    copy.wait_recv()

                    @pl.when(final)
                    def _():
                        acc[span, :] += inn[m].astype(F32)

                    @pl.when(jnp.logical_not(final))
                    def _():
                        out[m] = (partial[d, span, :] + inn[m].astype(F32)).astype(BF16)

                @pl.when(lag == 0)
                def _():
                    out[m] = partial[d, span, :].astype(BF16)

                @pl.when(jnp.logical_not(final))
                def _():
                    copy.start()

    relay_end = UNITS + SKEW * (LINE - 1)
    own_end = UNITS + SKEW * jnp.maximum(j, LINE - 1 - j)
    reduce_end = START + max(SPLIT * (LINE - k) + SKEW2 * k for k in range(LINE))

    def both(tau):
        @pl.when(tau == START)
        def _():
            backward()

        @pl.when(tau == own_end)
        def _():
            forward()

        relay_step(tau)
        reduce_step(tau - START)

    local_w.wait()
    run(max(relay_end + 1, reduce_end), both)
    dh_send[...] = acc[...].astype(BF16).reshape(NE, CAP, part)
    backs = spread(dh_send, dh_recv, d_ss, d_rs)
    others(lambda k: backs(k).start())
    local(5, dh_send.at[e], dh_recv.at[e]).start()

    local(2, own_h, h_all.at[y]).wait()
    local(3, out_send.at[e], out_recv.at[e]).wait()
    local(4, recv_g, g_all.at[y]).wait()
    local(5, dh_send.at[e], dh_recv.at[e]).wait()
    others(lambda k: grads(k).wait_send())
    others(lambda k: outs(k).wait_send())
    run(7, lambda k: near(k + 1).wait_send())

    @pl.when(last)
    def _():
        run(UNITS, lambda k: export(k, p_rs).wait_send())

    @pl.when(first)
    def _():
        run(UNITS, lambda k: export(k, m_rs).wait_send())

    @pl.when(j < LINE - 1)
    def _():
        run(UNITS, lambda u: relay(u, True).wait_send())
        run(SPLIT * (LINE - 1 - j), lambda m: passing(m, True).wait_send())

    @pl.when(j > 0)
    def _():
        run(UNITS, lambda u: relay(u, False).wait_send())
        run(SPLIT * j, lambda m: passing(m, False).wait_send())

    for d in (1, 2, 3):
        hid_y(d).wait_send()
        grad_y(d).wait_send()
        t = (y + d) % 4
        pltpu.make_async_copy(h_all.at[t], h_all.at[t], y_rs.at[t]).wait()
        pltpu.make_async_copy(g_all.at[t], g_all.at[t], y_rs.at[4 + t]).wait()
    others(arrivals(out_recv, o_rs))
    others(lambda k: backs(k).wait_send())
    others(arrivals(dh_recv, d_rs))


def shards(hidden, out_grad, w_down, routes, placement):
    experts = lax.axis_size("expert")
    replicas = lax.axis_size("dp")
    tok, width = hidden.shape
    cols = out_grad.shape[1]
    slots = experts * CAP
    part = width // LINE
    chosen = routes == jnp.arange(placement.shape[0], dtype=jnp.int32)[None, :]
    target = jnp.sum(jnp.where(chosen, placement[None, :], 0), axis=1)
    landing = target[:, None] == jnp.arange(experts, dtype=jnp.int32)[None, :]
    counted = jnp.cumsum(landing.astype(jnp.int32), axis=0) - 1
    within = jnp.sum(jnp.where(landing, counted, 0), axis=1)
    position = target * CAP + within
    picker = (jnp.arange(slots, dtype=jnp.int32)[:, None] == position[None, :]).astype(BF16)
    vmem = pl.BlockSpec(memory_space=pltpu.VMEM)
    dma = pltpu.SemaphoreType.DMA
    piece = (SPLIT * LINE, slots // SPLIT, part)
    back_out, back_grad, g_all, h_all = pl.pallas_call(
        exchange,
        out_shape=(
            jax.ShapeDtypeStruct((experts, CAP, cols), BF16),
            jax.ShapeDtypeStruct((experts, CAP, part), BF16),
            jax.ShapeDtypeStruct((replicas, experts, CAP, cols), BF16),
            jax.ShapeDtypeStruct((replicas, experts, CAP, width // replicas), BF16),
        ),
        in_specs=[vmem] * 3 + [pl.BlockSpec(memory_space=pl.ANY)],
        out_specs=(vmem,) * 4,
        scratch_shapes=[
            pltpu.VMEM((experts, CAP, width), BF16),
            pltpu.VMEM((experts, CAP, cols), BF16),
            pltpu.VMEM((width, cols), BF16),
            pltpu.VMEM((experts, CAP, width), BF16),
            pltpu.VMEM((experts, CAP, cols), BF16),
            pltpu.VMEM((experts, CAP, cols), BF16),
            pltpu.VMEM((experts, CAP, part), BF16),
            pltpu.VMEM((LINE, slots, part), F32),
            pltpu.VMEM((slots, part), F32),
            pltpu.VMEM(piece, BF16),
            pltpu.VMEM(piece, BF16),
            pltpu.VMEM(piece, BF16),
            pltpu.VMEM(piece, BF16),
            *[dma((NE,))] * 6,
            *[dma((8,))] * 2,
            *[dma((UNITS,))] * 5,
            *[dma((SPLIT * LINE,))] * 4,
            *[dma((8,))] * 2,
            dma((7,)),
        ],
        compiler_params=pltpu.CompilerParams(collective_id=0, has_side_effects=True, vmem_limit_bytes=60 * 2**20),
        name="exchange",
    )(hidden, out_grad, picker, w_down[0])
    output = jnp.einsum("rt,rd->td", picker, back_out.reshape(slots, cols), preferred_element_type=F32).astype(BF16)
    d_hidden = jnp.einsum("rt,rd->td", picker, back_grad.reshape(slots, part), preferred_element_type=F32).astype(BF16)
    d_weight = lax.dot_general(
        h_all.reshape(replicas * slots, -1),
        g_all.reshape(replicas * slots, cols),
        (((0,), (0,)), ((), ())),
        preferred_element_type=F32,
    ).astype(BF16)
    return (output, d_hidden, d_weight[None])


def solution(mesh):
    in_specs = (
        P(("dp", "expert"), None),
        P(("dp", "expert"), "tensor"),
        P("expert", None, "tensor"),
        P(("dp", "expert"), None),
        P(),
    )
    out_specs = (
        P(("dp", "expert"), "tensor"),
        P(("dp", "expert"), "tensor"),
        P("expert", "dp", "tensor"),
    )
    return jax.shard_map(shards, mesh=mesh, in_specs=in_specs, out_specs=out_specs, check_vma=False)
```
